32 devices in a mesh: frames: 4 (over y, x), tiles: 8 (over z, core).
Axes of the slice: x: 2, y: 2, z: 4, core: 2. Of those that a mesh axis runs over, the one named last changes fastest.
Arguments:
- features: bfloat16 [16, 64, 480, 128], P('frames', 'tiles'), may hold values from -6 to 6
- w_conv: bfloat16 [3, 3, 128, 128], replicated, may hold values from -0.1875 to 0.1875
- query_feats: bfloat16 [4096, 128], P(('frames', 'tiles')), may hold values from -6 to 6
- offset_rows: int32 [16, 32], P('frames'), may hold values from 0 to 7
- offset_cols: int32 [16, 32], P('frames'), may hold values from 0 to 471
- owners: int32 [32, 1], replicated, may hold values from 0 to 7; in each aligned block of 32 rows (0 to 31, 32 to 63, ...) at most 12 rows name the same one
- start_frames: int32 [4096], P(('frames', 'tiles')), may hold values from 0 to 15
- w_corr: bfloat16 [81, 384], replicated, may hold values from -0.625 to 0.625
- w_feat: bfloat16 [128, 384], replicated, may hold values from -0.5 to 0.5
- time_embed: float32 [16, 384], replicated, may hold values from -3 to 3
- gain_attn: float32 [384], replicated, may hold values from 0.5 to 1.5
- w_qkv: bfloat16 [384, 1152], replicated, may hold values from -1.0716518 to 1.0716518
- w_attn_out: bfloat16 [384, 384], replicated, may hold values from -0.3125 to 0.3125
- gain_mlp: float32 [384], replicated, may hold values from 0.5 to 1.5
- w_up: bfloat16 [384, 1536], replicated, may hold values from -0.3125 to 0.3125
- w_down: bfloat16 [1536, 384], replicated, may hold values from -0.15625 to 0.15625
Outputs:
- refined: bfloat16 [4096, 16, 384], P(('frames', 'tiles'))
The draws below stay inside these ranges and needn't reach their ends.
Inputs may be any that keep to these rules, and one draw needn't show every extreme that they name: `owners`: no tile owns more than 12 query blocks; some tile owns exactly 12; every tile owns at least one.
All inputs are finite; a program needn't handle non-finite values.
Results may differ from the reference program's by a relative error of at most 0.0066.
Values may be sent and summed in bfloat16 or wider, within the bound.
A program may use at most 192 MiB of HBM per device.

```python
import math
import jax
import jax.numpy as jnp
import numpy as np
from jax import lax

C = 128
D = 384
HEADS = 8
MLP_UNITS = 1536
WIN = 9
QBLK = 128
WIDTH_COLS = 480
TILE_ROWS = 8
FRAMES = 16
HEIGHT = 64
BLOCKS = 32
TRACKS = 4096
CAP = 12
N_TILES = 8


def draw_w_qkv(key, part):
    base = jnp.clip(jax.random.normal(jax.random.fold_in(key, 11), (D, 3 * D), jnp.float32), -3.5, 3.5) * D ** (-0.5)
    return base.astype(jnp.bfloat16)


def with_ends(values, rng, smallest, top_value):
    shape = values.shape
    spot = [jax.random.randint(jax.random.fold_in(rng, axis), (), 0, shape[axis]) for axis in range(len(shape))]
    values = values.at[tuple(spot)].set(smallest)
    longest = shape.index(max(shape))
    spot[longest] = (spot[longest] + 1) % shape[longest]
    return values.at[tuple(spot)].set(top_value)


def block_scale(key, extent, split, low, high):
    loudness = 1.0
    for axis_at, shards_of in split:
        heights = jax.random.uniform(jax.random.fold_in(jax.random.fold_in(key, 6), axis_at), (shards_of,), jnp.float32, low / len(split), high / len(split))
        loudness = loudness * jnp.repeat(jnp.exp(heights), extent[axis_at] // shards_of).reshape((-1,) + (1,) * (len(extent) - 1 - axis_at))
    return loudness


def routed_block(stream_key, own, number, rows, count, top, limit, lean):
    order = jax.random.permutation(stream_key, count)
    packed, common = shares(count, rows * top, limit, lean, True), shares(count, rows * top, limit, lean, False)
    places = jnp.arange(count)

    def named(sizes, rotation):
        used = int((sizes > 0).sum())
        fixed = max(1, used // 4)
        moved = fixed + (places - fixed + rotation * (used - fixed)) % max(1, count - fixed)
        return jnp.zeros((count,), jnp.int32).at[order[jnp.where(places < fixed, places, moved)]].set(jnp.asarray(sizes, jnp.int32))

    sizes = jnp.where(number % 4 == 0, named(packed, number // 4), named(common, number - number // 4 - 1))
    mixed = jax.random.permutation(jax.random.fold_in(own, 3), count)
    giver, sink = mixed[0:count // 2 * 2:2], mixed[1:count // 2 * 2:2]
    slack = jnp.minimum(sizes[giver] - 1, limit - sizes[sink]) // 2
    slack = jnp.where((giver == order[0]) | (sink == order[0]) | (sizes[sink] == 0), 0, jnp.maximum(slack, 0))
    moved = jax.random.randint(jax.random.fold_in(own, 4), (count // 2,), 0, 1 << 20) % (slack + 1)
    sizes = sizes.at[giver].add(-moved).at[sink].add(moved)
    members = jnp.searchsorted(jnp.cumsum(sizes), jnp.arange(rows * top), side="right").astype(jnp.int32)
    listing = members.reshape(top, rows).T
    listing = listing[jax.random.permutation(jax.random.fold_in(own, 1), rows)]
    rotation = jax.random.randint(jax.random.fold_in(own, 2), (rows, 1), 0, top)
    return jnp.take_along_axis(listing, (jnp.arange(top)[None, :] + rotation) % top, axis=1)


def shares(count, total, limit, slope, full):
    portions = [(1 << 20) // math.isqrt(rank ** slope) + 1 for rank in range(1, count + 1)]
    largest = limit if full else min(limit, max(-(-total // count), total * portions[0] // sum(portions)))
    least = 1 if total - largest >= count - 1 else 0
    given, surplus = [largest] + [least] * (count - 1), total - largest - least * (count - 1)
    while surplus > 0:
        free = [i for i in range(1, count) if given[i] < largest] or [i for i in range(1, count) if given[i] < limit]
        whole, remaining = sum([portions[i] for i in free]), surplus
        for i in free:
            addition = min(limit - given[i], max(1, remaining * portions[i] // whole), surplus)
            given[i] = given[i] + addition
            surplus = surplus - addition
    return np.array(given)


def noise(rng, extent, spread, most, cuts=(), held_as=jnp.bfloat16):
    level = block_scale(rng, extent, cuts, -0.22, 0.18) if cuts else 1.0
    entries = jax.random.normal(rng, extent, jnp.float32) * spread * level
    return jnp.minimum(jnp.maximum(entries, -most), most).astype(held_as)


def setup_inputs(seed: int = 0) -> dict:
    key_of = jax.random.split(jax.random.key(seed), 17)
    features = noise(key_of[0], (FRAMES, HEIGHT, WIDTH_COLS, C), 1.0, 6.0, ((0, 4), (1, 8)))
    w_conv = noise(key_of[1], (3, 3, C, C), (9 * C) ** -0.5, 0.1875)
    query_feats = noise(key_of[2], (TRACKS, C), 1.0, 6.0, ((0, 32),))
    offset_rows = with_ends(jax.random.randint(key_of[3], (FRAMES, BLOCKS), 0, TILE_ROWS), jax.random.fold_in(key_of[3], 1), 0, TILE_ROWS - 1).astype(jnp.int32)
    offset_cols = with_ends(jax.random.randint(key_of[4], (FRAMES, BLOCKS), 0, WIDTH_COLS - WIN + 1), jax.random.fold_in(key_of[4], 1), 0, WIDTH_COLS - WIN).astype(jnp.int32)
    owners_keys = jax.random.split(jax.random.fold_in(key_of[5], 1), BLOCKS // BLOCKS)
    owners_turns = jax.random.permutation(jax.random.fold_in(key_of[5], 3), BLOCKS // BLOCKS)
    owners = jax.vmap(lambda own, number: routed_block(jax.random.fold_in(key_of[5], 2), own, number, BLOCKS, N_TILES, 1, CAP, 2))(owners_keys, owners_turns).reshape((BLOCKS, 1))
    start_frames = with_ends(jax.random.randint(key_of[6], (TRACKS,), 0, FRAMES), jax.random.fold_in(key_of[6], 1), 0, FRAMES - 1).astype(jnp.int32)
    w_corr = noise(key_of[7], (WIN * WIN, D), (WIN * WIN) ** -0.5, 0.625)
    w_feat = noise(key_of[8], (C, D), C ** -0.5, 0.5)
    time_embed = noise(key_of[9], (FRAMES, D), 0.5, 3.0, (), jnp.float32)
    gain_attn = jnp.clip(1.0 + 0.1 * jax.random.normal(key_of[10], (D,), jnp.float32), 0.5, 1.5)
    w_qkv = draw_w_qkv(jax.random.fold_in(key_of[16], 71), 0)
    w_attn_out = noise(key_of[12], (D, D), D ** -0.5, 0.3125)
    gain_mlp = jnp.clip(1.0 + 0.1 * jax.random.normal(key_of[13], (D,), jnp.float32), 0.5, 1.5)
    w_up = noise(key_of[14], (D, MLP_UNITS), D ** -0.5, 0.3125)
    w_down = noise(key_of[15], (MLP_UNITS, D), MLP_UNITS ** -0.5, 0.15625)
    return {"features": features, "w_conv": w_conv, "query_feats": query_feats, "offset_rows": offset_rows, "offset_cols": offset_cols, "owners": owners, "start_frames": start_frames, "w_corr": w_corr, "w_feat": w_feat, "time_embed": time_embed, "gain_attn": gain_attn, "w_qkv": w_qkv, "w_attn_out": w_attn_out, "gain_mlp": gain_mlp, "w_up": w_up, "w_down": w_down}


def conv_frame(frame, w_conv):
    rows, cols, chans = frame.shape
    padded = jnp.pad(frame, ((1, 1), (1, 1), (0, 0)))
    total = jnp.zeros((rows * cols, chans), jnp.float32)
    for a in range(3):
        for b in range(3):
            piece = padded[a:a + rows, b:b + cols].reshape(rows * cols, chans)
            total = total + jnp.dot(piece, w_conv[a, b], preferred_element_type=jnp.float32)
    return total.reshape(rows, cols, chans).astype(jnp.bfloat16)

def rms_scale(values, gain):
    return values * lax.rsqrt(lax.optimization_barrier(jnp.mean(values * values, axis=-1, keepdims=True)) + 1e-06) * gain

def token_layer(tokens, starts, gain_attn, w_qkv, w_attn_out, gain_mlp, w_up, w_down):
    tracks, frames, width = tokens.shape
    head = width // HEADS
    normed = rms_scale(tokens, gain_attn).astype(jnp.bfloat16)
    qkv = jnp.einsum('tfd,de->tfe', normed.astype(jnp.float32), w_qkv.astype(jnp.float32)).astype(jnp.bfloat16)
    query = qkv[..., :width].reshape(tracks, frames, HEADS, head).astype(jnp.float32)
    keys = qkv[..., width:2 * width].reshape(tracks, frames, HEADS, head).astype(jnp.float32)
    values = qkv[..., 2 * width:].reshape(tracks, frames, HEADS, head).astype(jnp.float32)
    scores = jnp.einsum('tfhe,tghe->thfg', query, keys) * head ** (-0.5)
    valid = jnp.arange(frames)[None, :] >= starts[:, None]
    scores = jnp.where(valid[:, None, None, :], scores, -1e+30)
    top = lax.optimization_barrier(jnp.max(scores, axis=-1, keepdims=True))
    weights = jnp.exp(scores - top)
    probs = (weights / lax.optimization_barrier(jnp.sum(weights, axis=-1, keepdims=True))).astype(jnp.bfloat16)
    attended = jnp.einsum('thfg,tghe->tfhe', probs.astype(jnp.float32), values).astype(jnp.bfloat16)
    attended = attended.reshape(tracks, frames, width)
    mixed = tokens + jnp.einsum('tfd,de->tfe', attended.astype(jnp.float32), w_attn_out.astype(jnp.float32))
    normed2 = rms_scale(mixed, gain_mlp).astype(jnp.bfloat16)
    hidden = jax.nn.gelu(jnp.einsum('tfd,de->tfe', normed2.astype(jnp.float32), w_up.astype(jnp.float32)), approximate=True).astype(jnp.bfloat16)
    result = mixed + jnp.einsum('tfe,ed->tfd', hidden.astype(jnp.float32), w_down.astype(jnp.float32))
    return result.astype(jnp.bfloat16)

def reference(features, w_conv, query_feats, offset_rows, offset_cols, owners, start_frames, w_corr, w_feat, time_embed, gain_attn, w_qkv, w_attn_out, gain_mlp, w_up, w_down):
    chans = features.shape[-1]
    conv = lax.map(lambda frame: conv_frame(frame, w_conv), features)
    padded = jnp.pad(conv, ((0, 0), (4, 4), (0, 0), (0, 0)))
    queries = query_feats.reshape(-1, QBLK, chans)

    def frame_patch(frame, row, col):
        zero_start = jnp.zeros((), jnp.int32)
        return lax.dynamic_slice(frame, (row.astype(jnp.int32), col.astype(jnp.int32), zero_start), (WIN, WIN, chans)).reshape(WIN * WIN, chans)

    def block_corr(inputs):
        query, rows, cols, owner = inputs
        base = (owner * TILE_ROWS).astype(jnp.int32)
        patches = jax.vmap(frame_patch)(padded, (base + rows).astype(jnp.int32), cols.astype(jnp.int32))
        corr = jnp.einsum('fkc,qc->fkq', patches.astype(jnp.float32), query.astype(jnp.float32)) * chans ** (-0.5)
        return corr.astype(jnp.bfloat16)
    corr_all = lax.map(block_corr, (queries, offset_rows.T, offset_cols.T, owners[:, 0]))
    starts = start_frames.reshape(-1, QBLK)

    def block_tokens(inputs):
        corr, query, start = inputs
        tokens = jnp.einsum('fkq,kd->qfd', corr.astype(jnp.float32), w_corr.astype(jnp.float32))
        tokens = tokens + jnp.dot(query, w_feat, preferred_element_type=jnp.float32)[:, None, :] + time_embed[None]
        return token_layer(tokens, start, gain_attn, w_qkv, w_attn_out, gain_mlp, w_up, w_down)
    refined = lax.map(block_tokens, (corr_all, queries, starts))
    return refined.reshape(-1, refined.shape[2], refined.shape[3])
```

```python
import functools

import jax
import jax.numpy as jnp
from jax import lax
from jax.experimental import pallas as pl
from jax.experimental.pallas import tpu as pltpu
from jax.sharding import PartitionSpec as P

HEADS = 8
WIN = 9
QBLK = 128
CELLS = 96
REACH = WIN // 2
GROUP = 8
F32 = jnp.float32
BF16 = jnp.bfloat16
MESH = pl.DeviceIdType.MESH


def reversed_bits(value, bits):
    out = value * 0
    for bit in range(bits):
        out = out + ((value // 2**bit) % 2) * 2 ** (bits - 1 - bit)
    return out


def window_kernel(n_tiles, n_frames, owners, row_off, col_off, feat, w_cat, out, padded, conv, win):
    frame = pl.program_id(0)
    tile = lax.axis_index("tiles")
    rows, cols, chans = feat.shape[1:]
    blocks = owners.shape[0]
    per_group = blocks // n_frames
    blk_dev = per_group // n_tiles
    bits = n_tiles.bit_length() - 1

    @pl.when(frame == 0)
    def _():
        blank = jnp.zeros((2, cols, chans), BF16)
        padded[0:2] = blank
        padded[rows + 2 : rows + 4] = blank
        win[...] = jnp.zeros_like(win)
        conv[:, cols:] = jnp.zeros((rows + 2, 16, chans), F32)

    padded[2 : rows + 2] = feat[0]

    def conv_row(y, carry):
        wide = jnp.concatenate([padded[y], padded[y + 1], padded[y + 2]], axis=-1)
        parts = jnp.dot(wide, w_cat[...], preferred_element_type=F32)
        edge = jnp.zeros((1, chans), F32)
        left = jnp.concatenate([edge, parts[: cols - 1, :chans]], axis=0)
        right = jnp.concatenate([parts[1:, 2 * chans :], edge], axis=0)
        conv[y, :cols] = left + parts[:, chans : 2 * chans] + right
        return carry

    lax.fori_loop(0, rows + 2, conv_row, 0)

    def cut(block, carry):
        within = block % per_group
        slot = reversed_bits(within // blk_dev, bits)
        place = (block // per_group) * blk_dev + within % blk_dev
        owner = owners[block]
        first = owner * rows + row_off[frame, block] - REACH
        local = first - tile * rows
        touches = (local <= rows) & (local + WIN - 1 >= -1)

        @pl.when(touches)
        def _():
            col = col_off[frame, block]
            for i in range(WIN):
                row = local + i
                there = (row >= -1) & (row <= rows)
                there = there & (first + i >= 0) & (first + i < n_tiles * rows)
                cells = conv[jnp.clip(row + 1, 0, rows + 1), pl.ds(col, WIN), :]
                win[i * WIN : (i + 1) * WIN, :] = jnp.where(there, cells, 0.0)
            out[0, slot, place] = win[...].astype(BF16)

        @pl.when(jnp.logical_not(touches))
        def _():
            out[0, slot, place] = jnp.zeros((CELLS, chans), BF16)

        return carry

    lax.fori_loop(0, blocks, cut, 0)


def exchange_kernel(n_tiles, n_frames, parts, out, *scratch):
    levels = n_tiles.bit_length() - 1
    sums, lands = scratch[:levels], scratch[levels : 2 * levels]
    send_sem, recv_sem, out_send, out_recv = scratch[2 * levels :]
    tile, group = lax.axis_index("tiles"), lax.axis_index("frames")
    frame_dev = parts.shape[0]
    blk_dev = out.shape[1]

    partners = []
    for level in range(levels):
        bit = (tile // 2**level) % 2
        partners.append((group, tile + (1 - 2 * bit) * 2**level))
    peers = [((group + step) % n_frames, tile) for step in range(1, n_frames)]
    barrier = pltpu.get_barrier_semaphore()
    for device in partners + peers:
        pl.semaphore_signal(barrier, inc=1, device_id=device, device_id_type=MESH)
    pl.semaphore_wait(barrier, len(partners) + len(peers))

    def halving(level, frame):
        source = parts if level == 0 else sums[level - 1]
        count = n_tiles >> (level + 1)
        bit = (tile // 2**level) % 2
        copy = pltpu.make_async_remote_copy(
            src_ref=source.at[frame, pl.ds((1 - bit) * count, count)],
            dst_ref=lands[level].at[frame],
            send_sem=send_sem.at[level, frame],
            recv_sem=recv_sem.at[level, frame],
            device_id=partners[level],
            device_id_type=MESH,
        )
        return copy, source, bit * count, count

    pending = []
    for frame in range(frame_dev):
        halving(0, frame)[0].start()
    for level in range(levels):
        for frame in range(frame_dev):
            copy, source, start, count = halving(level, frame)
            copy.wait_recv()
            pending.append(copy)

            def add(i, carry):
                both = source[frame, start + i].astype(F32) + lands[level][frame, i].astype(F32)
                sums[level][frame, i] = both.astype(BF16)
                return carry

            lax.fori_loop(0, count, add, 0)
            if level + 1 < levels:
                halving(level + 1, frame)[0].start()
            else:
                for step, peer in enumerate(peers):
                    away = pltpu.make_async_remote_copy(
                        src_ref=sums[level].at[frame, 0, pl.ds(peer[0] * blk_dev, blk_dev)],
                        dst_ref=out.at[group * frame_dev + frame],
                        send_sem=out_send.at[step, frame],
                        recv_sem=out_recv.at[step, frame],
                        device_id=peer,
                        device_id_type=MESH,
                    )
                    away.start()
                out[group * frame_dev + frame] = sums[level][frame, 0, pl.ds(group * blk_dev, blk_dev)]
    for copy in pending:
        copy.wait_send()
    for step, peer in enumerate(peers):
        for frame in range(frame_dev):
            giver = (group + n_frames - step - 1) % n_frames
            pltpu.make_async_remote_copy(
                src_ref=sums[levels - 1].at[frame, 0, pl.ds(peer[0] * blk_dev, blk_dev)],
                dst_ref=out.at[giver * frame_dev + frame],
                send_sem=out_send.at[step, frame],
                recv_sem=out_recv.at[step, frame],
                device_id=peer,
                device_id_type=MESH,
            ).wait()


def rms_scale(values, gain):
    return values * lax.rsqrt(jnp.mean(values * values, axis=-1, keepdims=True) + 1e-06) * gain


def token_kernel(
    bundle, patch, query, starts, w_corr, w_feat, time_embed, gain_attn, w_qkv_t, w_attn_out, gain_mlp,
    w_up, w_down, out, tokens,
):
    step = pl.program_id(0)
    frames = patch.shape[0]
    chans = query.shape[1]
    width = w_feat.shape[1]
    head = width // HEADS
    span = GROUP * frames
    per_block = QBLK // (GROUP * bundle)

    @pl.when(step % per_block == 0)
    def _():
        queries = query[...]
        feat = jnp.dot(queries, w_feat[...], preferred_element_type=F32)
        for frame in range(frames):
            corr = lax.dot_general(
                patch[frame, 0], queries, (((1,), (1,)), ((), ())), preferred_element_type=F32
            ) * chans ** (-0.5)
            part = lax.dot_general(
                corr.astype(BF16), w_corr[...], (((0,), (0,)), ((), ())), preferred_element_type=F32
            )
            tokens[frame] = part + feat + time_embed[frame : frame + 1, :]

    first = (step % per_block) * (GROUP * bundle)
    x = jnp.concatenate(
        [
            tokens[:, pl.ds(pl.multiple_of(first + GROUP * g, GROUP), GROUP), :].reshape(span, width)
            for g in range(bundle)
        ],
        axis=0,
    )
    normed = rms_scale(x, gain_attn[...]).astype(BF16)
    qkv = lax.dot_general(
        w_qkv_t[...], normed, (((1,), (1,)), ((), ())), preferred_element_type=F32
    ).astype(BF16)
    key_at = lax.broadcasted_iota(jnp.int32, (span, span), 0)
    query_at = lax.broadcasted_iota(jnp.int32, (span, span), 1)
    same = (key_at % GROUP) == (query_at % GROUP)
    gathered = []
    for g in range(bundle):
        at = slice(g * span, (g + 1) * span)
        valid = same & ((key_at // GROUP) >= starts[0, g : g + 1, :])
        heads = []
        for h in range(HEADS):
            query_h = qkv[h * head : (h + 1) * head, at]
            key_h = qkv[width + h * head : width + (h + 1) * head, at]
            value_h = qkv[2 * width + h * head : 2 * width + (h + 1) * head, at]
            scores = lax.dot_general(
                key_h, query_h, (((0,), (0,)), ((), ())), preferred_element_type=F32
            ) * head ** (-0.5)
            scores = jnp.where(valid, scores, -1e30)
            weights = jnp.exp(scores - jnp.max(scores, axis=0, keepdims=True))
            total = jnp.sum(weights, axis=0, keepdims=True)
            mixed_h = jnp.dot(value_h, weights.astype(BF16), preferred_element_type=F32)
            heads.append((mixed_h / total).astype(BF16))
        gathered.append(jnp.concatenate(heads, axis=0))
    attended = jnp.concatenate(gathered, axis=1)
    mixed = x + lax.dot_general(
        attended, w_attn_out[...], (((0,), (0,)), ((), ())), preferred_element_type=F32
    )
    normed2 = rms_scale(mixed, gain_mlp[...]).astype(BF16)
    hidden = jax.nn.gelu(
        jnp.dot(normed2, w_up[...], preferred_element_type=F32), approximate=True
    ).astype(BF16)
    result = mixed + jnp.dot(hidden, w_down[...], preferred_element_type=F32)
    result = result.astype(BF16)
    move = (query_at == (key_at % frames) * GROUP + key_at // frames).astype(BF16)
    for g in range(bundle):
        at = slice(g * span, (g + 1) * span)
        out[at, :] = jnp.dot(move, result[at, :], preferred_element_type=F32).astype(BF16)


def body(
    features, w_conv, query_feats, offset_rows, offset_cols, owners, start_frames, w_corr, w_feat,
    time_embed, gain_attn, w_qkv, w_attn_out, gain_mlp, w_up, w_down,
):
    n_tiles = lax.axis_size("tiles")
    n_frames = lax.axis_size("frames")
    frame_dev, rows, cols, chans = features.shape
    blocks = owners.shape[0]
    blk_dev = blocks // (n_frames * n_tiles)
    lots = n_frames * blk_dev
    levels = n_tiles.bit_length() - 1
    frames_total = frame_dev * n_frames
    width = w_feat.shape[1]
    whole = pl.BlockSpec(memory_space=pltpu.VMEM)
    scalars = pl.BlockSpec(memory_space=pltpu.SMEM)

    w_cat = w_conv.transpose(0, 2, 1, 3).reshape(3 * chans, 3 * chans)
    parts = pl.pallas_call(
        functools.partial(window_kernel, n_tiles, n_frames),
        grid=(frame_dev,),
        out_shape=jax.ShapeDtypeStruct((frame_dev, n_tiles, lots, CELLS, chans), BF16),
        in_specs=[
            scalars,
            scalars,
            scalars,
            pl.BlockSpec((1, rows, cols, chans), lambda f: (f, 0, 0, 0)),
            pl.BlockSpec((3 * chans, 3 * chans), lambda f: (0, 0)),
        ],
        out_specs=pl.BlockSpec((1, n_tiles, lots, CELLS, chans), lambda f: (f, 0, 0, 0, 0)),
        scratch_shapes=[
            pltpu.VMEM((rows + 4, cols, chans), BF16),
            pltpu.VMEM((rows + 2, cols + 16, chans), F32),
            pltpu.VMEM((CELLS, chans), F32),
        ],
    )(owners[:, 0], offset_rows, offset_cols, features, w_cat)

    halves = [
        pltpu.VMEM((frame_dev, n_tiles >> (level + 1), lots, CELLS, chans), BF16)
        for level in range(levels)
    ]
    patch = pl.pallas_call(
        functools.partial(exchange_kernel, n_tiles, n_frames),
        out_shape=jax.ShapeDtypeStruct((frames_total, blk_dev, CELLS, chans), BF16),
        in_specs=[whole],
        out_specs=whole,
        scratch_shapes=halves
        + halves
        + [pltpu.SemaphoreType.DMA((levels, frame_dev))] * 2
        + [pltpu.SemaphoreType.DMA((n_frames - 1, frame_dev))] * 2,
        compiler_params=pltpu.CompilerParams(collective_id=0, has_side_effects=True),
    )(parts)

    bundle = 4
    span = GROUP * frames_total
    tracks = blk_dev * QBLK
    per_block = QBLK // (GROUP * bundle)
    starts = jnp.tile(start_frames.reshape(-1, bundle, GROUP), (1, 1, frames_total))
    w_corr_pad = jnp.pad(w_corr, ((0, CELLS - WIN * WIN), (0, 0)))

    def fixed(shape):
        return pl.BlockSpec(shape, lambda s: (0,) * len(shape))

    refined = pl.pallas_call(
        functools.partial(token_kernel, bundle),
        grid=(tracks // (GROUP * bundle),),
        out_shape=jax.ShapeDtypeStruct((tracks * frames_total, width), BF16),
        in_specs=[
            pl.BlockSpec((frames_total, 1, CELLS, chans), lambda s: (0, s // per_block, 0, 0)),
            pl.BlockSpec((QBLK, chans), lambda s: (s // per_block, 0)),
            pl.BlockSpec((1, bundle, span), lambda s: (s, 0, 0)),
            fixed((CELLS, width)),
            fixed(w_feat.shape),
            fixed(time_embed.shape),
            fixed((1, width)),
            fixed((3 * width, width)),
            fixed(w_attn_out.shape),
            fixed((1, width)),
            fixed(w_up.shape),
            fixed(w_down.shape),
        ],
        out_specs=pl.BlockSpec((bundle * span, width), lambda s: (s, 0)),
        scratch_shapes=[pltpu.VMEM((frames_total, QBLK, width), F32)],
    )(
        patch, query_feats, starts, w_corr_pad, w_feat, time_embed, gain_attn[None], w_qkv.T,
        w_attn_out, gain_mlp[None], w_up, w_down,
    )
    return refined.reshape(tracks, frames_total, width)


def solution(mesh):
    placed = (
        P("frames", "tiles", None, None),
        P(),
        P(("frames", "tiles"), None),
        P("frames", None),
        P("frames", None),
        P(),
        P(("frames", "tiles")),
    ) + (P(),) * 9
    return jax.shard_map(
        body,
        mesh=mesh,
        in_specs=placed,
        out_specs=P(("frames", "tiles"), None, None),
        check_vma=False,
    )
```

```python
import functools

import jax
import jax.numpy as jnp
from jax import lax
from jax.experimental import pallas as pl
from jax.experimental.pallas import tpu as pltpu
from jax.sharding import PartitionSpec as P

HEADS = 8
WIN = 9
QBLK = 128
CELLS = 96
REACH = WIN // 2
GROUP = 8
F32 = jnp.float32
BF16 = jnp.bfloat16
MESH = pl.DeviceIdType.MESH


def reversed_bits(value, bits):
    out = value * 0
    for bit in range(bits):
        out = out + ((value // 2**bit) % 2) * 2 ** (bits - 1 - bit)
    return out


def window_kernel(
    n_tiles, n_frames, owners, row_off, col_off, feat, w_conv, out, w_cat, padded, conv, win, parts, *scratch
):
    levels = n_tiles.bit_length() - 1
    sums, lands = scratch[:levels], scratch[levels : 2 * levels]
    feat_sem, send_sem, recv_sem, out_send, out_recv = scratch[2 * levels :]
    tile, group = lax.axis_index("tiles"), lax.axis_index("frames")
    frame_dev, rows, cols, chans = feat.shape
    blocks = owners.shape[0]
    per_group = blocks // n_frames
    blk_dev = out.shape[1]

    def fetch(frame):
        return pltpu.make_async_copy(feat.at[frame], padded.at[frame, pl.ds(2, rows)], feat_sem.at[frame])

    for frame in range(frame_dev):
        fetch(frame).start()
    partners = []
    for level in range(levels):
        bit = (tile // 2**level) % 2
        partners.append((group, tile + (1 - 2 * bit) * 2**level))
    peers = [((group + step) % n_frames, tile) for step in range(1, n_frames)]
    barrier = pltpu.get_barrier_semaphore()
    for device in partners + peers:
        pl.semaphore_signal(barrier, inc=1, device_id=device, device_id_type=MESH)

    blank = jnp.zeros((2, cols, chans), BF16)
    for frame in range(frame_dev):
        padded[frame, 0:2] = blank
        padded[frame, rows + 2 : rows + 4] = blank
    win[...] = jnp.zeros_like(win)
    conv[rows + 2] = jnp.zeros(conv.shape[1:], F32)
    conv[:, cols:] = jnp.zeros((rows + 3, conv.shape[1] - cols, chans), F32)
    for a in range(3):
        for b in range(3):
            w_cat[a * chans : (a + 1) * chans, b * chans : (b + 1) * chans] = w_conv[a, b]

    def halving(level, frame):
        source = parts if level == 0 else sums[level - 1]
        count = n_tiles >> (level + 1)
        bit = (tile // 2**level) % 2
        copy = pltpu.make_async_remote_copy(
            src_ref=source.at[frame, pl.ds((1 - bit) * count, count)],
            dst_ref=lands[level].at[frame],
            send_sem=send_sem.at[level, frame],
            recv_sem=recv_sem.at[level, frame],
            device_id=partners[level],
            device_id_type=MESH,
        )
        return copy, source, bit * count, count

    def handing(step, frame, giver):
        return pltpu.make_async_remote_copy(
            src_ref=sums[levels - 1].at[frame, 0, pl.ds(peers[step][0] * blk_dev, blk_dev)],
            dst_ref=out.at[giver * frame_dev + frame],
            send_sem=out_send.at[step, frame],
            recv_sem=out_recv.at[step, frame],
            device_id=peers[step],
            device_id_type=MESH,
        )

    def prepare(frame):
        fetch(frame).wait()

        def conv_row(y, carry):
            wide = jnp.concatenate([padded[frame, y], padded[frame, y + 1], padded[frame, y + 2]], axis=-1)
            sums_at = jnp.dot(wide, w_cat[...], preferred_element_type=F32)
            edge = jnp.zeros((1, chans), F32)
            left = jnp.concatenate([edge, sums_at[: cols - 1, :chans]], axis=0)
            right = jnp.concatenate([sums_at[1:, 2 * chans :], edge], axis=0)
            conv[y, :cols] = left + sums_at[:, chans : 2 * chans] + right
            return carry

        lax.fori_loop(0, rows + 2, conv_row, 0)

        def cut(slot, carry):
            within = reversed_bits(slot, levels)
            for group_at in range(n_frames):
                for extra in range(blk_dev):
                    block = group_at * per_group + within * blk_dev + extra
                    first = owners[block] * rows + row_off[frame, block] - REACH
                    local = first - tile * rows
                    col = col_off[frame, block]
                    for i in range(WIN):
                        row = local + i
                        there = (row >= -1) & (row <= rows)
                        there = there & (first + i >= 0) & (first + i < n_tiles * rows)
                        at = jnp.where(there, row + 1, rows + 2)
                        win[group_at * blk_dev + extra, i * WIN : (i + 1) * WIN, :] = conv[at, pl.ds(col, WIN), :]
            parts[frame, slot] = win[...].astype(BF16)
            return carry

        lax.fori_loop(0, n_tiles, cut, 0)

    def combine(level, frame):
        copy, source, start, count = halving(level, frame)
        copy.wait_recv()

        def add(i, carry):
            both = source[frame, start + i].astype(F32) + lands[level][frame, i].astype(F32)
            sums[level][frame, i] = both.astype(BF16)
            return carry

        lax.fori_loop(0, count, add, 0)
        if level + 1 < levels:
            halving(level + 1, frame)[0].start()
        else:
            for step in range(n_frames - 1):
                handing(step, frame, group).start()
            out[group * frame_dev + frame] = sums[level][frame, 0, pl.ds(group * blk_dev, blk_dev)]

    prepare(0)
    pl.semaphore_wait(barrier, len(partners) + len(peers))
    halving(0, 0)[0].start()

    def advance(turn, carry):
        @pl.when(turn < frame_dev)
        def _():
            prepare(turn)
            halving(0, turn)[0].start()

        for level in reversed(range(levels)):
            frame = turn - 1 - level

            @pl.when((frame >= 0) & (frame < frame_dev))
            def _():
                combine(level, frame)

        return carry

    lax.fori_loop(1, frame_dev + levels, advance, 0)
    for frame in range(frame_dev):
        for level in range(levels):
            halving(level, frame)[0].wait_send()
        for step in range(n_frames - 1):
            handing(step, frame, (group + n_frames - step - 1) % n_frames).wait()


def rms_scale(values, gain):
    return values * lax.rsqrt(jnp.mean(values * values, axis=-1, keepdims=True) + 1e-06) * gain


def token_kernel(
    bundle, patch, query, starts, w_corr, w_feat, time_embed, gain_attn, w_qkv_t, w_attn_out, gain_mlp,
    w_up, w_down, out, tokens,
):
    step = pl.program_id(0)
    frames = patch.shape[0]
    chans = query.shape[1]
    width = w_feat.shape[1]
    head = width // HEADS
    span = GROUP * frames
    per_block = QBLK // (GROUP * bundle)

    @pl.when(step % per_block == 0)
    def _():
        queries = query[...]
        feat = jnp.dot(queries, w_feat[...], preferred_element_type=F32)
        for frame in range(frames):
            corr = lax.dot_general(
                patch[frame, 0], queries, (((1,), (1,)), ((), ())), preferred_element_type=F32
            ) * chans ** (-0.5)
            part = lax.dot_general(
                corr.astype(BF16), w_corr[...], (((0,), (0,)), ((), ())), preferred_element_type=F32
            )
            tokens[frame] = part + feat + time_embed[frame : frame + 1, :]

    first = (step % per_block) * (GROUP * bundle)
    x = jnp.concatenate(
        [
            tokens[:, pl.ds(pl.multiple_of(first + GROUP * g, GROUP), GROUP), :].reshape(span, width)
            for g in range(bundle)
        ],
        axis=0,
    )
    normed = rms_scale(x, gain_attn[...]).astype(BF16)
    qkv = lax.dot_general(
        w_qkv_t[...], normed, (((1,), (1,)), ((), ())), preferred_element_type=F32
    ).astype(BF16)
    key_at = lax.broadcasted_iota(jnp.int32, (span, span), 0)
    query_at = lax.broadcasted_iota(jnp.int32, (span, span), 1)
    same = (key_at % GROUP) == (query_at % GROUP)
    gathered = []
    for g in range(bundle):
        at = slice(g * span, (g + 1) * span)
        valid = same & ((key_at // GROUP) >= starts[0, g : g + 1, :])
        heads = []
        for h in range(HEADS):
            query_h = qkv[h * head : (h + 1) * head, at]
            key_h = qkv[width + h * head : width + (h + 1) * head, at]
            value_h = qkv[2 * width + h * head : 2 * width + (h + 1) * head, at]
            scores = lax.dot_general(
                key_h, query_h, (((0,), (0,)), ((), ())), preferred_element_type=F32
            ) * head ** (-0.5)
            scores = jnp.where(valid, scores, -1e30)
            weights = jnp.exp(scores - jnp.max(scores, axis=0, keepdims=True))
            total = jnp.sum(weights, axis=0, keepdims=True)
            mixed_h = jnp.dot(value_h, weights.astype(BF16), preferred_element_type=F32)
            heads.append((mixed_h / total).astype(BF16))
        gathered.append(jnp.concatenate(heads, axis=0))
    attended = jnp.concatenate(gathered, axis=1)
    mixed = x + lax.dot_general(
        attended, w_attn_out[...], (((0,), (0,)), ((), ())), preferred_element_type=F32
    )
    normed2 = rms_scale(mixed, gain_mlp[...]).astype(BF16)
    hidden = jax.nn.gelu(
        jnp.dot(normed2, w_up[...], preferred_element_type=F32), approximate=True
    ).astype(BF16)
    result = mixed + jnp.dot(hidden, w_down[...], preferred_element_type=F32)
    result = result.astype(BF16)
    move = (query_at == (key_at % frames) * GROUP + key_at // frames).astype(BF16)
    for g in range(bundle):
        at = slice(g * span, (g + 1) * span)
        out[at, :] = jnp.dot(move, result[at, :], preferred_element_type=F32).astype(BF16)


def body(
    features, w_conv, query_feats, offset_rows, offset_cols, owners, start_frames, w_corr, w_feat,
    time_embed, gain_attn, w_qkv, w_attn_out, gain_mlp, w_up, w_down,
):
    n_tiles = lax.axis_size("tiles")
    n_frames = lax.axis_size("frames")
    frame_dev, rows, cols, chans = features.shape
    blocks = owners.shape[0]
    blk_dev = blocks // (n_frames * n_tiles)
    lots = n_frames * blk_dev
    levels = n_tiles.bit_length() - 1
    frames_total = frame_dev * n_frames
    width = w_feat.shape[1]
    whole = pl.BlockSpec(memory_space=pltpu.VMEM)
    scalars = pl.BlockSpec(memory_space=pltpu.SMEM)

    halves = [
        pltpu.VMEM((frame_dev, n_tiles >> (level + 1), lots, CELLS, chans), BF16)
        for level in range(levels)
    ]
    patch = pl.pallas_call(
        functools.partial(window_kernel, n_tiles, n_frames),
        out_shape=jax.ShapeDtypeStruct((frames_total, blk_dev, CELLS, chans), BF16),
        in_specs=[scalars, scalars, scalars, pl.BlockSpec(memory_space=pl.ANY), whole],
        out_specs=whole,
        scratch_shapes=[
            pltpu.VMEM((3 * chans, 3 * chans), BF16),
            pltpu.VMEM((frame_dev, rows + 4, cols, chans), BF16),
            pltpu.VMEM((rows + 3, cols + 16, chans), F32),
            pltpu.VMEM((lots, CELLS, chans), F32),
            pltpu.VMEM((frame_dev, n_tiles, lots, CELLS, chans), BF16),
        ]
        + halves
        + halves
        + [pltpu.SemaphoreType.DMA((frame_dev,))]
        + [pltpu.SemaphoreType.DMA((levels, frame_dev))] * 2
        + [pltpu.SemaphoreType.DMA((n_frames - 1, frame_dev))] * 2,
        compiler_params=pltpu.CompilerParams(collective_id=0, has_side_effects=True),
    )(owners[:, 0], offset_rows, offset_cols, features, w_conv)

    bundle = 4
    span = GROUP * frames_total
    tracks = blk_dev * QBLK
    per_block = QBLK // (GROUP * bundle)
    starts = jnp.tile(start_frames.reshape(-1, bundle, GROUP), (1, 1, frames_total))
    w_corr_pad = jnp.pad(w_corr, ((0, CELLS - WIN * WIN), (0, 0)))

    def fixed(shape):
        return pl.BlockSpec(shape, lambda s: (0,) * len(shape))

    refined = pl.pallas_call(
        functools.partial(token_kernel, bundle),
        grid=(tracks // (GROUP * bundle),),
        out_shape=jax.ShapeDtypeStruct((tracks * frames_total, width), BF16),
        in_specs=[
            pl.BlockSpec((frames_total, 1, CELLS, chans), lambda s: (0, s // per_block, 0, 0)),
            pl.BlockSpec((QBLK, chans), lambda s: (s // per_block, 0)),
            pl.BlockSpec((1, bundle, span), lambda s: (s, 0, 0)),
            fixed((CELLS, width)),
            fixed(w_feat.shape),
            fixed(time_embed.shape),
            fixed((1, width)),
            fixed((3 * width, width)),
            fixed(w_attn_out.shape),
            fixed((1, width)),
            fixed(w_up.shape),
            fixed(w_down.shape),
        ],
        out_specs=pl.BlockSpec((bundle * span, width), lambda s: (s, 0)),
        scratch_shapes=[pltpu.VMEM((frames_total, QBLK, width), F32)],
    )(
        patch, query_feats, starts, w_corr_pad, w_feat, time_embed, gain_attn[None], w_qkv.T,
        w_attn_out, gain_mlp[None], w_up, w_down,
    )
    return refined.reshape(tracks, frames_total, width)


def solution(mesh):
    placed = (
        P("frames", "tiles", None, None),
        P(),
        P(("frames", "tiles"), None),
        P("frames", None),
        P("frames", None),
        P(),
        P(("frames", "tiles")),
    ) + (P(),) * 9
    return jax.shard_map(
        body,
        mesh=mesh,
        in_specs=placed,
        out_specs=P(("frames", "tiles"), None, None),
        check_vma=False,
    )
```

```python
import functools
import math

import jax
import jax.numpy as jnp
from jax import lax
from jax.experimental import pallas as pl
from jax.experimental.pallas import tpu as pltpu
from jax.sharding import PartitionSpec as P

HEADS = 8
WIN = 9
QBLK = 128
CELLS = 96
REACH = WIN // 2
GROUP = 8
F32 = jnp.float32
BF16 = jnp.bfloat16
MESH = pl.DeviceIdType.MESH


def reversed_bits(value, bits):
    out = value * 0
    for bit in range(bits):
        out = out + ((value // 2**bit) % 2) * 2 ** (bits - 1 - bit)
    return out


def window_kernel(
    n_tiles, n_frames, owners, row_off, col_off, feat, w_conv, out, w_cat, padded, conv, win, parts, *scratch
):
    levels = n_tiles.bit_length() - 1
    sums, lands = scratch[:levels], scratch[levels : 2 * levels]
    feat_sem, send_sem, recv_sem, out_send, out_recv = scratch[2 * levels :]
    tile, group = lax.axis_index("tiles"), lax.axis_index("frames")
    frame_dev, rows, cols, chans = feat.shape
    blocks = owners.shape[0]
    per_group = blocks // n_frames
    blk_dev = out.shape[1]

    def fetch(frame):
        return pltpu.make_async_copy(feat.at[frame], padded.at[frame, pl.ds(2, rows)], feat_sem.at[frame])

    for frame in range(frame_dev):
        fetch(frame).start()
    partners = []
    for level in range(levels):
        bit = (tile // 2**level) % 2
        partners.append((group, tile + (1 - 2 * bit) * 2**level))
    peers = [((group + step) % n_frames, tile) for step in range(1, n_frames)]
    barrier = pltpu.get_barrier_semaphore()
    for device in partners + peers:
        pl.semaphore_signal(barrier, inc=1, device_id=device, device_id_type=MESH)

    blank = jnp.zeros((2, cols, chans), BF16)
    for frame in range(frame_dev):
        padded[frame, 0:2] = blank
        padded[frame, rows + 2 : rows + 4] = blank
    win[...] = jnp.zeros_like(win)
    for y in range(WIN):
        conv[y] = jnp.zeros(conv.shape[1:], F32)
        conv[WIN + rows + 2 + y] = jnp.zeros(conv.shape[1:], F32)
    conv[WIN : WIN + rows + 2, cols:] = jnp.zeros((rows + 2, conv.shape[1] - cols, chans), F32)
    for a in range(3):
        for b in range(3):
            w_cat[a * chans : (a + 1) * chans, b * chans : (b + 1) * chans] = w_conv[a, b]

    def halving(level, frame):
        source = parts if level == 0 else sums[level - 1]
        count = n_tiles >> (level + 1)
        bit = (tile // 2**level) % 2
        copy = pltpu.make_async_remote_copy(
            src_ref=source.at[frame, pl.ds((1 - bit) * count, count)],
            dst_ref=lands[level].at[frame],
            send_sem=send_sem.at[level, frame],
            recv_sem=recv_sem.at[level, frame],
            device_id=partners[level],
            device_id_type=MESH,
        )
        return copy, source, bit * count, count

    def handing(step, frame, giver):
        return pltpu.make_async_remote_copy(
            src_ref=sums[levels - 1].at[frame, 0, pl.ds(peers[step][0] * blk_dev, blk_dev)],
            dst_ref=out.at[giver * frame_dev + frame],
            send_sem=out_send.at[step, frame],
            recv_sem=out_recv.at[step, frame],
            device_id=peers[step],
            device_id_type=MESH,
        )

    def prepare(frame):
        fetch(frame).wait()

        def conv_rows(pair, carry):
            for half in range(2):
                y = 2 * pair + half
                wide = jnp.concatenate([padded[frame, y], padded[frame, y + 1], padded[frame, y + 2]], axis=-1)
                sums_at = jnp.dot(wide, w_cat[...], preferred_element_type=F32)
                edge = jnp.zeros((1, chans), F32)
                left = jnp.concatenate([edge, sums_at[: cols - 1, :chans]], axis=0)
                right = jnp.concatenate([sums_at[1:, 2 * chans :], edge], axis=0)
                conv[WIN + y, :cols] = left + sums_at[:, chans : 2 * chans] + right
            return carry

        lax.fori_loop(0, (rows + 2) // 2, conv_rows, 0)

        @pl.when(tile == 0)
        def _():
            conv[WIN, :cols] = jnp.zeros((cols, chans), F32)

        @pl.when(tile == n_tiles - 1)
        def _():
            conv[WIN + rows + 1, :cols] = jnp.zeros((cols, chans), F32)

        def cut(slot, carry):
            within = reversed_bits(slot, levels)
            for group_at in range(n_frames):
                for extra in range(blk_dev):
                    block = group_at * per_group + within * blk_dev + extra
                    local = (owners[block] - tile) * rows + row_off[frame, block] - REACH
                    first = jnp.clip(local + 1, -WIN, rows + 2) + WIN
                    col = col_off[frame, block]
                    lot = group_at * blk_dev + extra
                    for i in range(WIN):
                        win[lot, i * WIN : (i + 1) * WIN, :] = conv[first + i, pl.ds(col, WIN), :]
            parts[frame, slot] = win[...].astype(BF16)
            return carry

        lax.fori_loop(0, n_tiles, cut, 0)

    def combine(level, frame):
        copy, source, start, count = halving(level, frame)
        copy.wait_recv()

        def add(i, carry):
            both = source[frame, start + i].astype(F32) + lands[level][frame, i].astype(F32)
            sums[level][frame, i] = both.astype(BF16)
            return carry

        lax.fori_loop(0, count, add, 0)
        if level + 1 < levels:
            halving(level + 1, frame)[0].start()
        else:
            for step in range(n_frames - 1):
                handing(step, frame, group).start()
            out[group * frame_dev + frame] = sums[level][frame, 0, pl.ds(group * blk_dev, blk_dev)]

    prepare(0)
    pl.semaphore_wait(barrier, len(partners) + len(peers))
    halving(0, 0)[0].start()

    def advance(turn, carry):
        @pl.when(turn < frame_dev)
        def _():
            prepare(turn)
            halving(0, turn)[0].start()

        for level in reversed(range(levels)):
            frame = turn - 1 - level

            @pl.when((frame >= 0) & (frame < frame_dev))
            def _():
                combine(level, frame)

        return carry

    lax.fori_loop(1, frame_dev + levels, advance, 0)
    for frame in range(frame_dev):
        for level in range(levels):
            halving(level, frame)[0].wait_send()
        for step in range(n_frames - 1):
            handing(step, frame, (group + n_frames - step - 1) % n_frames).wait()


def rms_scale(values, gain):
    return values * lax.rsqrt(jnp.mean(values * values, axis=-1, keepdims=True) + 1e-06) * gain


def token_kernel(
    bundle, patch, query, starts, w_corr, w_feat, time_embed, gain_attn, w_qkv, w_attn_out, gain_mlp,
    w_up, w_down, out, tokens, w_token, w_qkv_t,
):
    step = pl.program_id(0)
    frames, _, cells, chans = patch.shape
    width = w_feat.shape[1]
    head = width // HEADS
    span = GROUP * frames
    per_block = QBLK // (GROUP * bundle)

    @pl.when(step == 0)
    def _():
        w_token[:chans] = jnp.zeros((chans, width), BF16)
        w_token[: w_corr.shape[0]] = w_corr[...]
        w_token[chans:] = w_feat[...]
        w_qkv_t[...] = w_qkv[...].T

    @pl.when(step % per_block == 0)
    def _():
        queries = query[...]
        blank = jnp.zeros((chans - cells, chans), BF16)
        for some in range(0, frames, 4):
            corrs = []
            for frame in range(some, some + 4):
                window = jnp.concatenate([patch[frame, 0], blank], axis=0)
                corr = lax.dot_general(
                    queries, window, (((1,), (1,)), ((), ())), preferred_element_type=F32
                ) * chans ** (-0.5)
                corrs.append(jnp.concatenate([corr.astype(BF16), queries], axis=1))
            made = jnp.dot(jnp.concatenate(corrs, axis=0), w_token[...], preferred_element_type=F32)
            for n in range(4):
                tokens[some + n] = made[n * QBLK : (n + 1) * QBLK] + time_embed[some + n : some + n + 1, :]

    first = (step % per_block) * (GROUP * bundle)
    x = jnp.concatenate(
        [
            tokens[:, pl.ds(pl.multiple_of(first + GROUP * g, GROUP), GROUP), :].reshape(span, width)
            for g in range(bundle)
        ],
        axis=0,
    )
    normed = rms_scale(x, gain_attn[...]).astype(BF16)
    qkv = lax.dot_general(
        w_qkv_t[...], normed, (((1,), (1,)), ((), ())), preferred_element_type=F32
    ).astype(BF16)
    key_at = lax.broadcasted_iota(jnp.int32, (span, span), 0)
    query_at = lax.broadcasted_iota(jnp.int32, (span, span), 1)
    same = (key_at % GROUP) == (query_at % GROUP)
    power = head ** (-0.5) * math.log2(math.e)
    start_rows = jnp.broadcast_to(starts[...].astype(F32)[None, :], (GROUP, QBLK)).astype(BF16)
    source = lax.broadcasted_iota(jnp.int32, (QBLK, span), 0)
    track = lax.broadcasted_iota(jnp.int32, (QBLK, span), 1) % GROUP
    gathered = []
    for g in range(bundle):
        at = slice(g * span, (g + 1) * span)
        pick = (source == track + (first + GROUP * g)).astype(BF16)
        start = jnp.dot(start_rows, pick, preferred_element_type=F32)[:1].astype(jnp.int32)
        valid = same & ((key_at // GROUP) >= start)
        scores = [
            lax.dot_general(
                qkv[width + h * head : width + (h + 1) * head, at],
                qkv[h * head : (h + 1) * head, at],
                (((0,), (0,)), ((), ())),
                preferred_element_type=F32,
            )
            for h in range(HEADS)
        ]
        weights, totals = [], []
        for h in range(HEADS):
            score = jnp.where(valid, scores[h], -1e30)
            weight = jnp.exp2((score - jnp.max(score, axis=0, keepdims=True)) * power)
            totals.append(jnp.sum(weight, axis=0, keepdims=True))
            weights.append(weight.astype(BF16))
        heads = [
            jnp.dot(
                qkv[2 * width + h * head : 2 * width + (h + 1) * head, at],
                weights[h],
                preferred_element_type=F32,
            )
            for h in range(HEADS)
        ]
        gathered.append(
            jnp.concatenate([(heads[h] / totals[h]).astype(BF16) for h in range(HEADS)], axis=0)
        )
    attended = jnp.concatenate(gathered, axis=1)
    mixed = x + lax.dot_general(
        attended, w_attn_out[...], (((0,), (0,)), ((), ())), preferred_element_type=F32
    )
    normed2 = rms_scale(mixed, gain_mlp[...]).astype(BF16)
    hidden = jax.nn.gelu(
        jnp.dot(normed2, w_up[...], preferred_element_type=F32), approximate=True
    ).astype(BF16)
    result = mixed + jnp.dot(hidden, w_down[...], preferred_element_type=F32)
    result = result.astype(BF16)
    move = (query_at == (key_at % frames) * GROUP + key_at // frames).astype(BF16)
    for g in range(bundle):
        at = slice(g * span, (g + 1) * span)
        out[at, :] = jnp.dot(move, result[at, :], preferred_element_type=F32).astype(BF16)


def body(
    features, w_conv, query_feats, offset_rows, offset_cols, owners, start_frames, w_corr, w_feat,
    time_embed, gain_attn, w_qkv, w_attn_out, gain_mlp, w_up, w_down,
):
    n_tiles = lax.axis_size("tiles")
    n_frames = lax.axis_size("frames")
    frame_dev, rows, cols, chans = features.shape
    blocks = owners.shape[0]
    blk_dev = blocks // (n_frames * n_tiles)
    lots = n_frames * blk_dev
    levels = n_tiles.bit_length() - 1
    frames_total = frame_dev * n_frames
    width = w_feat.shape[1]
    whole = pl.BlockSpec(memory_space=pltpu.VMEM)
    scalars = pl.BlockSpec(memory_space=pltpu.SMEM)

    halves = [
        pltpu.VMEM((frame_dev, n_tiles >> (level + 1), lots, CELLS, chans), BF16)
        for level in range(levels)
    ]
    patch = pl.pallas_call(
        functools.partial(window_kernel, n_tiles, n_frames),
        out_shape=jax.ShapeDtypeStruct((frames_total, blk_dev, CELLS, chans), BF16),
        in_specs=[scalars, scalars, scalars, pl.BlockSpec(memory_space=pl.ANY), whole],
        out_specs=whole,
        scratch_shapes=[
            pltpu.VMEM((3 * chans, 3 * chans), BF16),
            pltpu.VMEM((frame_dev, rows + 4, cols, chans), BF16),
            pltpu.VMEM((rows + 2 + 2 * WIN, cols + 16, chans), F32),
            pltpu.VMEM((lots, CELLS, chans), F32),
            pltpu.VMEM((frame_dev, n_tiles, lots, CELLS, chans), BF16),
        ]
        + halves
        + halves
        + [pltpu.SemaphoreType.DMA((frame_dev,))]
        + [pltpu.SemaphoreType.DMA((levels, frame_dev))] * 2
        + [pltpu.SemaphoreType.DMA((n_frames - 1, frame_dev))] * 2,
        compiler_params=pltpu.CompilerParams(collective_id=0, has_side_effects=True),
    )(owners[:, 0], offset_rows, offset_cols, features, w_conv)

    bundle = 4
    span = GROUP * frames_total
    tracks = blk_dev * QBLK
    per_block = QBLK // (GROUP * bundle)
    def fixed(shape):
        return pl.BlockSpec(shape, lambda s: (0,) * len(shape))

    refined = pl.pallas_call(
        functools.partial(token_kernel, bundle),
        grid=(tracks // (GROUP * bundle),),
        out_shape=jax.ShapeDtypeStruct((tracks * frames_total, width), BF16),
        in_specs=[
            pl.BlockSpec((frames_total, 1, CELLS, chans), lambda s: (0, s // per_block, 0, 0)),
            pl.BlockSpec((QBLK, chans), lambda s: (s // per_block, 0)),
            pl.BlockSpec((QBLK,), lambda s: (s // per_block,)),
            fixed(w_corr.shape),
            fixed(w_feat.shape),
            fixed(time_embed.shape),
            fixed((width,)),
            fixed(w_qkv.shape),
            fixed(w_attn_out.shape),
            fixed((width,)),
            fixed(w_up.shape),
            fixed(w_down.shape),
        ],
        out_specs=pl.BlockSpec((bundle * span, width), lambda s: (s, 0)),
        scratch_shapes=[
            pltpu.VMEM((frames_total, QBLK, width), F32),
            pltpu.VMEM((2 * chans, width), BF16),
            pltpu.VMEM((3 * width, width), BF16),
        ],
    )(
        patch, query_feats, start_frames, w_corr, w_feat, time_embed, gain_attn, w_qkv,
        w_attn_out, gain_mlp, w_up, w_down,
    )
    return refined.reshape(tracks, frames_total, width)


def solution(mesh):
    placed = (
        P("frames", "tiles", None, None),
        P(),
        P(("frames", "tiles"), None),
        P("frames", None),
        P("frames", None),
        P(),
        P(("frames", "tiles")),
    ) + (P(),) * 9
    return jax.shard_map(
        body,
        mesh=mesh,
        in_specs=placed,
        out_specs=P(("frames", "tiles"), None, None),
        check_vma=False,
    )
```

```python
import functools
import math

import jax
import jax.numpy as jnp
from jax import lax
from jax.experimental import pallas as pl
from jax.experimental.pallas import tpu as pltpu
from jax.sharding import PartitionSpec as P

HEADS = 8
WIN = 9
QBLK = 128
CELLS = 88
REACH = WIN // 2
GROUP = 8
F32 = jnp.float32
BF16 = jnp.bfloat16
MESH = pl.DeviceIdType.MESH


def reversed_bits(value, bits):
    out = value * 0
    for bit in range(bits):
        out = out + ((value // 2**bit) % 2) * 2 ** (bits - 1 - bit)
    return out


def window_kernel(
    n_tiles, n_frames, owners, row_off, col_off, feat, w_conv, out, w_cat, padded, conv, win, parts, *scratch
):
    levels = n_tiles.bit_length() - 1
    sums, lands = scratch[:levels], scratch[levels : 2 * levels]
    feat_sem, send_sem, recv_sem, out_send, out_recv = scratch[2 * levels :]
    tile, group = lax.axis_index("tiles"), lax.axis_index("frames")
    frame_dev, rows, cols, chans = feat.shape
    blocks = owners.shape[0]
    per_group = blocks // n_frames
    blk_dev = out.shape[1]

    def fetch(frame):
        return pltpu.make_async_copy(feat.at[frame], padded.at[frame, pl.ds(2, rows)], feat_sem.at[frame])

    for frame in range(frame_dev):
        fetch(frame).start()
    partners = []
    for level in range(levels):
        bit = (tile // 2**level) % 2
        partners.append((group, tile + (1 - 2 * bit) * 2**level))
    peers = [((group + step) % n_frames, tile) for step in range(1, n_frames)]
    barrier = pltpu.get_barrier_semaphore()
    for device in partners + peers:
        pl.semaphore_signal(barrier, inc=1, device_id=device, device_id_type=MESH)

    blank = jnp.zeros((2, cols, chans), BF16)
    for frame in range(frame_dev):
        padded[frame, 0:2] = blank
        padded[frame, rows + 2 : rows + 4] = blank
    win[...] = jnp.zeros_like(win)
    for y in range(WIN):
        conv[y] = jnp.zeros(conv.shape[1:], F32)
        conv[WIN + rows + 2 + y] = jnp.zeros(conv.shape[1:], F32)
    conv[WIN : WIN + rows + 2, cols:] = jnp.zeros((rows + 2, conv.shape[1] - cols, chans), F32)
    for a in range(3):
        for b in range(3):
            w_cat[a * chans : (a + 1) * chans, b * chans : (b + 1) * chans] = w_conv[a, b]

    def halving(level, frame):
        source = parts if level == 0 else sums[level - 1]
        count = n_tiles >> (level + 1)
        bit = (tile // 2**level) % 2
        copy = pltpu.make_async_remote_copy(
            src_ref=source.at[frame, pl.ds((1 - bit) * count, count)],
            dst_ref=lands[level].at[frame],
            send_sem=send_sem.at[level, frame],
            recv_sem=recv_sem.at[level, frame],
            device_id=partners[level],
            device_id_type=MESH,
        )
        return copy, source, bit * count, count

    def handing(step, frame, giver):
        return pltpu.make_async_remote_copy(
            src_ref=sums[levels - 1].at[frame, 0, pl.ds(peers[step][0] * blk_dev, blk_dev)],
            dst_ref=out.at[giver * frame_dev + frame],
            send_sem=out_send.at[step, frame],
            recv_sem=out_recv.at[step, frame],
            device_id=peers[step],
            device_id_type=MESH,
        )

    def convolve(frame):
        fetch(frame).wait()

        def conv_rows(pair, carry):
            for half in range(2):
                y = 2 * pair + half
                wide = jnp.concatenate([padded[frame, y], padded[frame, y + 1], padded[frame, y + 2]], axis=-1)
                sums_at = jnp.dot(wide, w_cat[...], preferred_element_type=F32)
                edge = jnp.zeros((1, chans), F32)
                left = jnp.concatenate([edge, sums_at[: cols - 1, :chans]], axis=0)
                right = jnp.concatenate([sums_at[1:, 2 * chans :], edge], axis=0)
                conv[WIN + y, :cols] = left + sums_at[:, chans : 2 * chans] + right
            return carry

        lax.fori_loop(0, (rows + 2) // 2, conv_rows, 0)

        @pl.when(tile == 0)
        def _():
            conv[WIN, :cols] = jnp.zeros((cols, chans), F32)

        @pl.when(tile == n_tiles - 1)
        def _():
            conv[WIN + rows + 1, :cols] = jnp.zeros((cols, chans), F32)

    def cut_all(frame):
        def cut(slot, carry):
            within = reversed_bits(slot, levels)
            for group_at in range(n_frames):
                for extra in range(blk_dev):
                    block = group_at * per_group + within * blk_dev + extra
                    local = (owners[block] - tile) * rows + row_off[frame, block] - REACH
                    first = jnp.clip(local + 1, -WIN, rows + 2) + WIN
                    col = col_off[frame, block]
                    lot = group_at * blk_dev + extra
                    for i in range(WIN):
                        win[lot, i * WIN : (i + 1) * WIN, :] = conv[first + i, pl.ds(col, WIN), :]
            parts[frame, slot] = win[...].astype(BF16)
            return carry

        lax.fori_loop(0, n_tiles, cut, 0)

    def combine(level, frame):
        copy, source, start, count = halving(level, frame)
        copy.wait_recv()

        def add(i, carry):
            both = source[frame, start + i].astype(F32) + lands[level][frame, i].astype(F32)
            sums[level][frame, i] = both.astype(BF16)
            return carry

        lax.fori_loop(0, count, add, 0)
        if level + 1 < levels:
            halving(level + 1, frame)[0].start()
        else:
            for step in range(n_frames - 1):
                handing(step, frame, group).start()
            out[group * frame_dev + frame] = sums[level][frame, 0, pl.ds(group * blk_dev, blk_dev)]

    convolve(0)
    cut_all(0)
    pl.semaphore_wait(barrier, len(partners) + len(peers))
    halving(0, 0)[0].start()

    def advance(turn, carry):
        @pl.when(turn < frame_dev)
        def _():
            convolve(turn)

        @pl.when(turn <= frame_dev)
        def _():
            combine(0, turn - 1)

        @pl.when(turn < frame_dev)
        def _():
            cut_all(turn)
            halving(0, turn)[0].start()

        for level in reversed(range(1, levels)):
            frame = turn - 1 - level

            @pl.when((frame >= 0) & (frame < frame_dev))
            def _():
                combine(level, frame)

        return carry

    lax.fori_loop(1, frame_dev + levels, advance, 0)
    for frame in range(frame_dev):
        for level in range(levels):
            halving(level, frame)[0].wait_send()
        for step in range(n_frames - 1):
            handing(step, frame, (group + n_frames - step - 1) % n_frames).wait()


def rms_scale(values, gain):
    return values * lax.rsqrt(jnp.mean(values * values, axis=-1, keepdims=True) + 1e-06) * gain


def token_kernel(
    bundle, patch, query, starts, w_corr, w_feat, time_embed, gain_attn, w_qkv, w_attn_out, gain_mlp,
    w_up, w_down, out, tokens, w_token, w_qkv_t,
):
    step = pl.program_id(0)
    frames, _, cells, chans = patch.shape
    width = w_feat.shape[1]
    head = width // HEADS
    span = GROUP * frames
    per_block = QBLK // (GROUP * bundle)

    @pl.when(step == 0)
    def _():
        w_token[:chans] = jnp.zeros((chans, width), BF16)
        w_token[: w_corr.shape[0]] = w_corr[...]
        w_token[chans:] = w_feat[...]
        w_qkv_t[...] = w_qkv[...].T

    @pl.when(step % per_block == 0)
    def _():
        queries = query[...]
        blank = jnp.zeros((chans - cells, chans), BF16)
        for some in range(0, frames, 4):
            corrs = []
            for frame in range(some, some + 4):
                window = jnp.concatenate([patch[frame, 0], blank], axis=0)
                corr = lax.dot_general(
                    queries, window, (((1,), (1,)), ((), ())), preferred_element_type=F32
                ) * chans ** (-0.5)
                corrs.append(jnp.concatenate([corr.astype(BF16), queries], axis=1))
            made = jnp.dot(jnp.concatenate(corrs, axis=0), w_token[...], preferred_element_type=F32)
            for n in range(4):
                tokens[some + n] = made[n * QBLK : (n + 1) * QBLK] + time_embed[some + n : some + n + 1, :]

    first = (step % per_block) * (GROUP * bundle)
    x = jnp.concatenate(
        [
            tokens[:, pl.ds(pl.multiple_of(first + GROUP * g, GROUP), GROUP), :].reshape(span, width)
            for g in range(bundle)
        ],
        axis=0,
    )
    normed = rms_scale(x, gain_attn[...]).astype(BF16)
    qkv = lax.dot_general(
        w_qkv_t[...], normed, (((1,), (1,)), ((), ())), preferred_element_type=F32
    ).astype(BF16)
    key_at = lax.broadcasted_iota(jnp.int32, (span, span), 0)
    query_at = lax.broadcasted_iota(jnp.int32, (span, span), 1)
    same = (key_at % GROUP) == (query_at % GROUP)
    power = head ** (-0.5) * math.log2(math.e)
    start_rows = jnp.broadcast_to(starts[...].astype(F32)[None, :], (GROUP, QBLK)).astype(BF16)
    source = lax.broadcasted_iota(jnp.int32, (QBLK, span), 0)
    track = lax.broadcasted_iota(jnp.int32, (QBLK, span), 1) % GROUP
    gathered = []
    for g in range(bundle):
        at = slice(g * span, (g + 1) * span)
        pick = (source == track + (first + GROUP * g)).astype(BF16)
        start = jnp.dot(start_rows, pick, preferred_element_type=F32)[:1].astype(jnp.int32)
        valid = same & ((key_at // GROUP) >= start)
        scores = [
            lax.dot_general(
                qkv[width + h * head : width + (h + 1) * head, at],
                qkv[h * head : (h + 1) * head, at],
                (((0,), (0,)), ((), ())),
                preferred_element_type=F32,
            )
            for h in range(HEADS)
        ]
        weights, totals = [], []
        for h in range(HEADS):
            score = jnp.where(valid, scores[h], -1e30)
            weight = jnp.exp2((score - jnp.max(score, axis=0, keepdims=True)) * power)
            totals.append(jnp.sum(weight, axis=0, keepdims=True))
            weights.append(weight.astype(BF16))
        heads = [
            jnp.dot(
                qkv[2 * width + h * head : 2 * width + (h + 1) * head, at],
                weights[h],
                preferred_element_type=F32,
            )
            for h in range(HEADS)
        ]
        gathered.append(
            jnp.concatenate([(heads[h] / totals[h]).astype(BF16) for h in range(HEADS)], axis=0)
        )
    attended = jnp.concatenate(gathered, axis=1)
    mixed = x + lax.dot_general(
        attended, w_attn_out[...], (((0,), (0,)), ((), ())), preferred_element_type=F32
    )
    normed2 = rms_scale(mixed, gain_mlp[...]).astype(BF16)
    hidden = jax.nn.gelu(
        jnp.dot(normed2, w_up[...], preferred_element_type=F32), approximate=True
    ).astype(BF16)
    result = mixed + jnp.dot(hidden, w_down[...], preferred_element_type=F32)
    result = result.astype(BF16)
    move = (query_at == (key_at % frames) * GROUP + key_at // frames).astype(BF16)
    for g in range(bundle):
        at = slice(g * span, (g + 1) * span)
        out[at, :] = jnp.dot(move, result[at, :], preferred_element_type=F32).astype(BF16)


def body(
    features, w_conv, query_feats, offset_rows, offset_cols, owners, start_frames, w_corr, w_feat,
    time_embed, gain_attn, w_qkv, w_attn_out, gain_mlp, w_up, w_down,
):
    n_tiles = lax.axis_size("tiles")
    n_frames = lax.axis_size("frames")
    frame_dev, rows, cols, chans = features.shape
    blocks = owners.shape[0]
    blk_dev = blocks // (n_frames * n_tiles)
    lots = n_frames * blk_dev
    levels = n_tiles.bit_length() - 1
    frames_total = frame_dev * n_frames
    width = w_feat.shape[1]
    whole = pl.BlockSpec(memory_space=pltpu.VMEM)
    scalars = pl.BlockSpec(memory_space=pltpu.SMEM)

    halves = [
        pltpu.VMEM((frame_dev, n_tiles >> (level + 1), lots, CELLS, chans), BF16)
        for level in range(levels)
    ]
    patch = pl.pallas_call(
        functools.partial(window_kernel, n_tiles, n_frames),
        out_shape=jax.ShapeDtypeStruct((frames_total, blk_dev, CELLS, chans), BF16),
        in_specs=[scalars, scalars, scalars, pl.BlockSpec(memory_space=pl.ANY), whole],
        out_specs=whole,
        scratch_shapes=[
            pltpu.VMEM((3 * chans, 3 * chans), BF16),
            pltpu.VMEM((frame_dev, rows + 4, cols, chans), BF16),
            pltpu.VMEM((rows + 2 + 2 * WIN, cols + 16, chans), F32),
            pltpu.VMEM((lots, CELLS, chans), F32),
            pltpu.VMEM((frame_dev, n_tiles, lots, CELLS, chans), BF16),
        ]
        + halves
        + halves
        + [pltpu.SemaphoreType.DMA((frame_dev,))]
        + [pltpu.SemaphoreType.DMA((levels, frame_dev))] * 2
        + [pltpu.SemaphoreType.DMA((n_frames - 1, frame_dev))] * 2,
        compiler_params=pltpu.CompilerParams(collective_id=0, has_side_effects=True),
    )(owners[:, 0], offset_rows, offset_cols, features, w_conv)

    bundle = 4
    span = GROUP * frames_total
    tracks = blk_dev * QBLK
    per_block = QBLK // (GROUP * bundle)
    def fixed(shape):
        return pl.BlockSpec(shape, lambda s: (0,) * len(shape))

    refined = pl.pallas_call(
        functools.partial(token_kernel, bundle),
        grid=(tracks // (GROUP * bundle),),
        out_shape=jax.ShapeDtypeStruct((tracks * frames_total, width), BF16),
        in_specs=[
            pl.BlockSpec((frames_total, 1, CELLS, chans), lambda s: (0, s // per_block, 0, 0)),
            pl.BlockSpec((QBLK, chans), lambda s: (s // per_block, 0)),
            pl.BlockSpec((QBLK,), lambda s: (s // per_block,)),
            fixed(w_corr.shape),
            fixed(w_feat.shape),
            fixed(time_embed.shape),
            fixed((width,)),
            fixed(w_qkv.shape),
            fixed(w_attn_out.shape),
            fixed((width,)),
            fixed(w_up.shape),
            fixed(w_down.shape),
        ],
        out_specs=pl.BlockSpec((bundle * span, width), lambda s: (s, 0)),
        scratch_shapes=[
            pltpu.VMEM((frames_total, QBLK, width), F32),
            pltpu.VMEM((2 * chans, width), BF16),
            pltpu.VMEM((3 * width, width), BF16),
        ],
    )(
        patch, query_feats, start_frames, w_corr, w_feat, time_embed, gain_attn, w_qkv,
        w_attn_out, gain_mlp, w_up, w_down,
    )
    return refined.reshape(tracks, frames_total, width)


def solution(mesh):
    placed = (
        P("frames", "tiles", None, None),
        P(),
        P(("frames", "tiles"), None),
        P("frames", None),
        P("frames", None),
        P(),
        P(("frames", "tiles")),
    ) + (P(),) * 9
    return jax.shard_map(
        body,
        mesh=mesh,
        in_specs=placed,
        out_specs=P(("frames", "tiles"), None, None),
        check_vma=False,
    )
```
